32 devices in a mesh: leaf: 8 (over z, core), leg: 4 (over y, x).
Axes of the slice: x: 2, y: 2, z: 4, core: 2. Of those that a mesh axis runs over, the one named last changes fastest.
Arguments:
- tensor_low: bfloat16 [8, 256, 256, 256], P('leaf', None, 'leg'), may hold values from -0.0234375 to 0.0234375
- tensor_mid: bfloat16 [8, 256, 128, 256], P('leaf', None, 'leg'), may hold values from -0.0234375 to 0.0234375
- tensor_top: bfloat16 [8, 256, 64, 256], P('leaf', None, 'leg'), may hold values from -0.0234375 to 0.0234375
- child_operators: bfloat16 [8, 2, 4, 256, 256], P('leaf'), may hold values from -6 to 6
- term_choice: int32 [8, 2, 2], P('leaf'), may hold values from 0 to 3
Outputs:
- top_operators: float32 [8, 2, 64, 256], P('leaf', None, 'leg')
The draws below stay inside these ranges and needn't reach their ends.
All inputs are finite; a program needn't handle non-finite values.
Results may differ from the reference program's by a relative error of at most 0.019.
Values may be sent and summed in bfloat16 or wider, within the bound.
No kernel may reach another device: no remote copies, remote signals or barrier semaphores. Data moves between devices by JAX's collectives and lax.ppermute only.
A program may use at most 128 MiB of HBM per device.

```python
import jax
import jax.numpy as jnp
from jax import lax

BOND = 256
KOPS = 4
NODES_A = 8
NODES_B = 4
NODES_C = 2
N_LEG = 4


def plant(values, own_key, smallest, high):
    longest = values.shape.index(max(values.shape))
    spots = []
    for shift in (0, 1):
        where = [jax.random.randint(jax.random.fold_in(own_key, axis), (), 0, length) for axis, length in enumerate(values.shape)]
        where[longest] = (where[longest] + shift) % values.shape[longest]
        spots.append(tuple(where))
    return values.at[spots[0]].set(smallest).at[spots[1]].set(high)


def levels(key, shape, split, smallest, high):
    gain, own = 1.0, jax.random.fold_in(key, 6)
    for axis_at, parts in split:
        heights = jnp.exp(jax.random.uniform(jax.random.fold_in(own, axis_at), (parts,), jnp.float32, smallest / len(split), high / len(split)))
        gain = gain * jnp.repeat(heights, shape[axis_at] // parts).reshape([-1 if axis == axis_at else 1 for axis in range(len(shape))])
    return gain


def bell_draw(key, shape, scale, reach, cuts=(), held_as=jnp.bfloat16):
    result = jax.random.normal(key, shape, jnp.float32) * scale
    if len(cuts) > 0:
        result = levels(key, shape, cuts, -0.22, 0.18) * result
    return jnp.clip(result, min=-reach, max=reach).astype(held_as)


def setup_inputs(seed: int = 0) -> dict:
    streams_of = jax.random.split(jax.random.key(seed), 6)
    tensor_low = bell_draw(streams_of[0], (NODES_A, BOND, BOND, BOND), (BOND * BOND) ** -0.5, 0.0234375, ((0, 8), (2, 4)))
    tensor_mid = bell_draw(streams_of[1], (2 * NODES_B, BOND, BOND // 2, BOND), (BOND * BOND) ** -0.5, 0.0234375, ((0, 8), (2, 4)))
    tensor_top = bell_draw(streams_of[2], (4 * NODES_C, BOND, BOND // 4, BOND), (BOND * BOND) ** -0.5, 0.0234375, ((0, 8), (2, 4)))
    child_operators = bell_draw(streams_of[3], (NODES_A, 2, KOPS, BOND, BOND), 1.0, 6.0, ((0, 8),))
    term_choice = plant(jax.random.randint(streams_of[4], (NODES_A, 2, 2), 0, KOPS), jax.random.fold_in(streams_of[4], 1), 0, KOPS - 1).astype(jnp.int32)
    return {"tensor_low": tensor_low, "tensor_mid": tensor_mid, "tensor_top": tensor_top, "child_operators": child_operators, "term_choice": term_choice}


def assemble(blocked):
    parts_count, bond_size, part_width, depth_size = blocked.shape
    slice_width = part_width // N_LEG
    arranged = blocked.reshape(parts_count, bond_size, N_LEG, slice_width, depth_size)
    arranged = jnp.transpose(arranged, (1, 2, 0, 3, 4))
    return arranged.reshape(bond_size, parts_count * part_width, depth_size)


def renormalize(tensor, left_operator, operator_on_right):
    broad_tensor = tensor.astype(jnp.float32)
    blended_terms = jnp.einsum('lm,lra->mra', left_operator.astype(jnp.float32), broad_tensor).astype(jnp.bfloat16)
    rotated_tensor = jnp.einsum('tbe,bw->twe', blended_terms.astype(jnp.float32), operator_on_right.astype(jnp.float32)).astype(jnp.bfloat16)
    return jnp.einsum('orc,orh->ch', rotated_tensor.astype(jnp.float32), broad_tensor)


def renormalize_level(stored, left_ops, right_ops, parts_count):
    node_count = stored.shape[0] // parts_count
    blocked = stored.reshape((node_count, parts_count) + stored.shape[1:])

    def per_node(node_items):
        block_of_nodes, left_node, right_node = node_items
        tensor = assemble(block_of_nodes)
        return jnp.stack([renormalize(tensor, left_node[term_index], right_node[term_index]) for term_index in range(2)])

    return lax.map(per_node, (blocked, left_ops, right_ops))


def select_operators(operator_bank, chosen_operators):
    return jnp.stack([jnp.stack([operator_bank[side_index][chosen_operators[term_index, side_index]] for side_index in range(2)]) for term_index in range(2)])


def reference(tensor_low, tensor_mid, tensor_top, child_operators, term_choice):
    paired = jax.vmap(select_operators)(child_operators, term_choice)
    level_low = renormalize_level(tensor_low, paired[:, :, 0], paired[:, :, 1], 1).astype(jnp.bfloat16)
    level_mid = renormalize_level(tensor_mid, level_low[0::2], level_low[1::2], 2).astype(jnp.bfloat16)
    level_top = renormalize_level(tensor_top, level_mid[0::2], level_mid[1::2], 4)
    node_count = level_top.shape[0]
    bond_size = level_top.shape[-1]
    arranged = level_top.reshape(node_count, 2, 4, bond_size // 4, bond_size)
    arranged = jnp.transpose(arranged, (0, 2, 1, 3, 4))
    return arranged.reshape(node_count * 4, 2, bond_size // 4, bond_size)
```

```python
import functools

import jax
import jax.numpy as jnp
from jax import lax
from jax.experimental import pallas as pl
from jax.experimental.pallas import tpu as pltpu
from jax.sharding import PartitionSpec as P

F32 = jnp.float32
BF16 = jnp.bfloat16
LANES = 128
VMEM_BYTES = 56 << 20
AXES = ("leaf", "leg")


def from_partner(block, axis, apart):
    count = lax.axis_size(axis)
    route = []
    for low in range(count):
        high = low | 1 << apart
        if high != low and high < count:
            route += [(low, high), (high, low)]
    return lax.ppermute(block, axis, route)


def regroup(stacked, leaf_flag_bits, leg_count):
    stacked_count, bond_size, row_count, feature_width = stacked.shape
    group_size = 2 ** len(leaf_flag_bits)
    slice_width = bond_size // (leg_count * group_size)
    shaped = stacked.reshape(
        stacked_count, leg_count, group_size, slice_width, 1, row_count, feature_width
    )
    leaf_index = lax.axis_index("leaf")
    for leaf_bit in leaf_flag_bits:
        own_bit = leaf_index >> leaf_bit & 1
        dims_now = shaped.shape
        halves = shaped.reshape(dims_now[:2] + (2, dims_now[2] // 2) + dims_now[3:])
        kept_half = lax.dynamic_index_in_dim(halves, own_bit, 2, keepdims=False)
        sent_half = lax.dynamic_index_in_dim(halves, 1 - own_bit, 2, keepdims=False)
        partner = from_partner(sent_half, "leaf", leaf_bit)
        lower_half = jnp.where(own_bit == 0, kept_half, partner)
        upper_half = jnp.where(own_bit == 0, partner, kept_half)
        joined = jnp.stack([lower_half, upper_half], axis=5)
        shaped = joined.reshape(
            dims_now[:2] + (dims_now[2] // 2, dims_now[3], dims_now[4] * 2) + dims_now[5:]
        )
    flattened = shaped.reshape(
        stacked_count, leg_count, slice_width, group_size * row_count, feature_width
    )
    regrouped = lax.all_to_all(flattened, "leg", split_axis=1, concat_axis=3, tiled=True)
    return regrouped.reshape(stacked_count, slice_width, bond_size, feature_width)


def contract_left(left_ops, tensor):
    return jnp.einsum("tlm,lra->tmra", left_ops, tensor, preferred_element_type=F32).astype(BF16)


def renormalize_level(tensor, left_ops, right_ops, leaf_flag_bits, leg_count):
    shifted_tensor = regroup(tensor[None], leaf_flag_bits, leg_count)[0]
    left_mixed = contract_left(left_ops, tensor)
    mixed_moved = regroup(left_mixed, leaf_flag_bits, leg_count)
    rotated_tensor = jnp.einsum(
        "tkra,trs->tkas", mixed_moved, right_ops, preferred_element_type=F32
    ).astype(BF16)
    partial_value = jnp.einsum(
        "tkas,ksb->tab", rotated_tensor, shifted_tensor, preferred_element_type=F32
    )
    totals = lax.psum(partial_value, "leg")
    for leaf_bit in leaf_flag_bits:
        totals = totals + from_partner(totals, "leaf", leaf_bit)
    return totals


def pair_children(operators, leaf_bit):
    side_bit = lax.axis_index("leaf") >> leaf_bit & 1
    partner = from_partner(operators, "leaf", leaf_bit)
    return (
        jnp.where(side_bit == 0, operators, partner),
        jnp.where(side_bit == 0, partner, operators),
    )


def choose_operators(operator_bank, chosen_operators, term_count):
    return [
        jnp.stack(
            [
                lax.dynamic_index_in_dim(
                    operator_bank[side], chosen_operators[term, side], 0, keepdims=False
                )
                for term in range(term_count)
            ]
        )
        for side in range(2)
    ]


def on_any_mesh(tensor_low, tensor_mid, tensor_top, child_operators, term_choice):
    leg_count = lax.axis_size("leg")
    leaf_index = lax.axis_index("leaf")
    left_ops, right_ops = choose_operators(child_operators[0], term_choice[0], term_choice.shape[1])
    level_low = renormalize_level(tensor_low[0], left_ops, right_ops, [], leg_count).astype(BF16)
    bond_size = level_low.shape[-1]
    quarter = bond_size // 4
    row_count = quarter // leg_count
    row_start = (leaf_index & 3) * quarter + lax.axis_index("leg") * row_count
    left_ops, right_ops = pair_children(level_low, 0)
    level_mid = renormalize_level(tensor_mid[0], left_ops, right_ops, [0], leg_count).astype(BF16)
    left_ops, right_ops = pair_children(level_mid, 1)
    level_top = renormalize_level(tensor_top[0], left_ops, right_ops, [1, 0], leg_count)
    return lax.dynamic_slice_in_dim(level_top, row_start, row_count, 1)[None]


def mix_kernel(chunk, w_ref, l_ref, o_ref, lt_ref, *scratch):
    depth, _, width = w_ref.shape
    terms = l_ref.shape[0]
    rows = terms * depth
    pieces = width // LANES
    wide, out = scratch[:pieces], scratch[pieces:]

    @pl.when(pl.program_id(0) == 0)
    def _():
        for t in range(terms):
            lt_ref[t * depth : (t + 1) * depth, :] = l_ref[t].astype(F32).T.astype(BF16)

    for h in range(pieces):
        lanes = slice(h * LANES, (h + 1) * LANES)
        wide[h][...] = w_ref[:, :, lanes].astype(F32).reshape(depth * chunk, LANES)
    for r in range(chunk):
        slab = jnp.concatenate(
            [wide[h][pl.ds(r, depth, stride=chunk), :].astype(BF16) for h in range(pieces)], axis=1
        )
        mixed = jnp.dot(lt_ref[...], slab, preferred_element_type=F32)
        for h in range(pieces):
            out[h][pl.ds(r, rows, stride=chunk), :] = mixed[:, h * LANES : (h + 1) * LANES]
    for h in range(pieces):
        lanes = slice(h * LANES, (h + 1) * LANES)
        value = out[h][...].reshape(terms, depth, chunk, LANES).astype(BF16)
        o_ref[:, :, :, lanes] = value


def mix(block, left_ops, chunk=8):
    depth, count, width = block.shape
    terms = left_ops.shape[0]
    pieces = width // LANES
    return pl.pallas_call(
        functools.partial(mix_kernel, chunk),
        out_shape=jax.ShapeDtypeStruct((terms, depth, count, width), BF16),
        grid=(count // chunk,),
        in_specs=[
            pl.BlockSpec((depth, chunk, width), lambda i: (0, i, 0)),
            pl.BlockSpec(left_ops.shape, lambda i: (0, 0, 0)),
        ],
        out_specs=pl.BlockSpec((terms, depth, chunk, width), lambda i: (0, 0, i, 0)),
        scratch_shapes=[pltpu.VMEM((terms * depth, depth), BF16)]
        + [pltpu.VMEM((depth * chunk, LANES), F32)] * pieces
        + [pltpu.VMEM((terms * depth * chunk, LANES), F32)] * pieces,
        compiler_params=pltpu.CompilerParams(vmem_limit_bytes=VMEM_BYTES),
        cost_estimate=pl.CostEstimate(
            flops=3 * 2 * terms * depth * depth * count * width,
            bytes_accessed=(1 + terms) * 2 * depth * count * width,
            transcendentals=0,
        ),
    )(block, left_ops)


def combine_kernel(block_count, mixed_count, group, *refs):
    blocks = refs[:block_count]
    mixed = refs[block_count : block_count + mixed_count]
    r_ref, rows_ref, columns_ref, o_ref, turn_ref = refs[block_count + mixed_count :]
    terms, step = mixed[0].shape[:2]
    own = turn_ref.shape[0] // terms

    @pl.when(pl.program_id(0) == 0)
    def _():
        o_ref[...] = jnp.zeros_like(o_ref)
        for t in range(terms):
            picked = jnp.dot(rows_ref[...], r_ref[t], preferred_element_type=F32).astype(BF16)
            turn_ref[t * own : (t + 1) * own, :] = jnp.dot(
                picked, columns_ref[...], preferred_element_type=F32
            ).astype(BF16)

    for start in range(0, step, group):
        members = range(start, start + group)
        turned = []
        for m in members:
            whole = jnp.concatenate([block[m] for block in blocks], axis=0)
            turned.append(
                jnp.dot(turn_ref[...], whole, preferred_element_type=F32).astype(BF16)
            )
        for t in range(terms):
            left = jnp.concatenate([x[t, m] for m in members for x in mixed], axis=0)
            right = jnp.concatenate([y[t * own : (t + 1) * own] for y in turned], axis=0)
            o_ref[t] += lax.dot_general(
                left, right, (((0,), (0,)), ((), ())), preferred_element_type=F32
            )


def combine(blocks, mixed, right_ops, row_pick, column_pick, step=32, group=8):
    depth, _, width = blocks[0].shape
    terms = right_ops.shape[0]
    own = row_pick.shape[0]
    return pl.pallas_call(
        functools.partial(combine_kernel, len(blocks), len(mixed), group),
        out_shape=jax.ShapeDtypeStruct((terms, width, width), F32),
        grid=(depth // step,),
        in_specs=[pl.BlockSpec((step,) + b.shape[1:], lambda i: (i, 0, 0)) for b in blocks]
        + [pl.BlockSpec((terms, step) + x.shape[2:], lambda i: (0, i, 0, 0)) for x in mixed]
        + [
            pl.BlockSpec(right_ops.shape, lambda i: (0, 0, 0)),
            pl.BlockSpec(row_pick.shape, lambda i: (0, 0)),
            pl.BlockSpec(column_pick.shape, lambda i: (0, 0)),
        ],
        out_specs=pl.BlockSpec((terms, width, width), lambda i: (0, 0, 0)),
        scratch_shapes=[pltpu.VMEM((terms * own, depth), BF16)],
        compiler_params=pltpu.CompilerParams(vmem_limit_bytes=VMEM_BYTES),
        cost_estimate=pl.CostEstimate(
            flops=2 * terms * own * depth * width * (depth + width),
            bytes_accessed=2 * depth * width * (depth + terms * own),
            transcendentals=0,
        ),
    )(*blocks, *mixed, right_ops, row_pick, column_pick)


def move(array, route):
    leg_count = lax.axis_size("leg")
    pairs = [(a * leg_count + g, b * leg_count + h) for (a, g), (b, h) in route.items()]
    return lax.ppermute(array, AXES, pairs)


def hop(array, start, end):
    return move(array, {(n, start): (n, end) for n in range(lax.axis_size("leaf"))})


def gather(x_part, y_part, straight_part, bent_part, sinks):
    leaves = range(lax.axis_size("leaf"))

    def toward(array, start, end):
        return move(array, {(n, s ^ start): (n, s ^ end) for n in leaves for s in sinks})

    bent = toward(bent_part, 3, 1)
    near_x = toward(x_part, 1, 0)
    near_y = toward(y_part, 2, 0)
    straight = toward(straight_part, 3, 0)
    bent = toward(bent, 1, 0)
    return near_x, near_y, straight, bent


def share(arrays, sinks):
    leaves = range(lax.axis_size("leaf"))
    return [move(a, {(n, s): (n ^ 1, s) for n in leaves for s in sinks}) for a in arrays]


def add_core(partial, sinks):
    return (partial + share([partial], sinks)[0]).astype(BF16)


def picks(index, own):
    size = index.shape[0]
    canonical = jnp.arange(size)
    rows = (index[:own, None] == canonical[None, :]).astype(BF16)
    columns = (canonical[:, None] == index[None, :]).astype(BF16)
    return rows, columns


def order(bond_size, parts, leg_count, own_part, legs):
    width = bond_size // (leg_count * len(parts))
    place = jnp.arange(bond_size)
    part_at = place // (leg_count * width)
    part = sum(jnp.where(part_at == i, own_part ^ p, 0) for i, p in enumerate(parts))
    leg_at = place // width % leg_count
    leg = sum(jnp.where(leg_at == i, g, 0) for i, g in enumerate(legs))
    return leg * (bond_size // leg_count) + part * width + place % width


def halves(block):
    middle = block.shape[1] // 2
    return block[:, :middle], block[:, middle:]


def on_square(tensor_low, tensor_mid, tensor_top, child_operators, term_choice):
    leaf, leg = lax.axis_index("leaf"), lax.axis_index("leg")
    leaf_count, leg_count = lax.axis_size("leaf"), lax.axis_size("leg")
    leaves, legs = range(leaf_count), range(leg_count)
    low, mid, top = tensor_low[0], tensor_mid[0], tensor_top[0]
    bond_size = low.shape[-1]
    core = leaf & 1
    low_sinks, mid_sinks, top_sinks = (0, 3), (1,), (2,)

    half = low.shape[1] // 2
    own_half = lax.dynamic_slice_in_dim(low, core * half, half, 1)
    sent_half = lax.dynamic_slice_in_dim(low, (1 - core) * half, half, 1)
    got_half = lax.ppermute(sent_half, "leaf", [(n, n ^ 1) for n in leaves])
    own_first = (core == 0) == (leg < 2)
    first = jnp.where(own_first, own_half, got_half)
    second = jnp.where(own_first, got_half, own_half)
    straight_part, bent_part = halves(second)
    column = [first, *gather(first, second, straight_part, bent_part, low_sinks)]
    low_blocks = column + share(column, low_sinks)

    left_ops, right_ops = choose_operators(child_operators[0], term_choice[0], term_choice.shape[1])
    foreign = core != leg // 2
    ops_pair = jnp.stack([left_ops, right_ops])
    other_pair = lax.ppermute(ops_pair, "leaf", [(n, n ^ 1) for n in leaves])
    left_ops, right_ops = jnp.where(foreign, other_pair, ops_pair)

    low_legs = [leg, leg ^ 1, leg ^ 2, leg ^ 3]
    row_pick, column_pick = picks(
        order(bond_size, (0, 1), leg_count, core, low_legs), bond_size // 2
    )
    mixed = [mix(block, left_ops) for block in column]
    ops_low = add_core(combine(low_blocks, mixed, right_ops, row_pick, column_pick), low_sinks)

    straight_part, bent_part = halves(mid)
    column = [mid, *gather(mid, mid, straight_part, bent_part, mid_sinks)]
    mid_blocks = column + share(column, mid_sinks)
    left_ops = move(ops_low, {(n, low_sinks[0]): (n, mid_sinks[0]) for n in leaves})
    right_ops = move(ops_low, {(n, low_sinks[1]): (n, mid_sinks[0]) for n in leaves})
    row_pick, column_pick = picks(
        order(bond_size, (0, 1), leg_count, core, [mid_sinks[0] ^ d for d in range(4)]),
        bond_size // 2,
    )
    mixed = [mix(block, left_ops) for block in column]
    ops_mid = add_core(combine(mid_blocks, mixed, right_ops, row_pick, column_pick), mid_sinks)

    sink = top_sinks[0]
    other = lax.ppermute(top, "leaf", [(n, n ^ 2) for n in leaves])
    column = [top, hop(top, sink ^ 1, sink), hop(top, sink ^ 2, sink), hop(top, sink ^ 3, sink)]
    bent = hop(other, sink ^ 3, sink ^ 1)
    column += [other, hop(other, sink ^ 1, sink), hop(other, sink ^ 2, sink), hop(bent, sink ^ 1, sink)]
    top_blocks = column + share(column, top_sinks)
    near = hop(ops_mid, mid_sinks[0], sink)
    across = move(ops_mid, {(n, mid_sinks[0]): (n ^ 2, sink) for n in leaves})
    upper = (leaf >> 1 & 1) == 1
    left_ops, right_ops = jnp.where(upper, across, near), jnp.where(upper, near, across)
    row_pick, column_pick = picks(
        order(bond_size, (0, 2, 1, 3), leg_count, leaf & 3, [sink ^ d for d in range(4)]),
        bond_size // 4,
    )
    mixed = [mix(block, left_ops) for block in column[:4]]
    partial = combine(top_blocks, mixed, right_ops, row_pick, column_pick)

    quarter = bond_size // 4
    summed = lax.dynamic_slice_in_dim(partial, (leaf & 3) * quarter, quarter, 1)
    for apart in (1, 2, 3):
        piece = lax.dynamic_slice_in_dim(partial, ((leaf & 3) ^ apart) * quarter, quarter, 1)
        summed = summed + move(piece, {(n, sink): (n ^ apart, sink) for n in leaves})
    rows = quarter // leg_count
    result = jnp.where(leg == sink, summed[:, sink * rows : (sink + 1) * rows], 0)
    for g in legs:
        if g != sink:
            result = result + hop(summed[:, g * rows : (g + 1) * rows], sink, g)
    return result[None]


def on_device(*arguments):
    if lax.axis_size("leg") == 4 and lax.axis_size("leaf") % 4 == 0:
        return on_square(*arguments)
    return on_any_mesh(*arguments)


def solution(mesh):
    return jax.shard_map(
        on_device,
        mesh=mesh,
        in_specs=(
            P("leaf", None, "leg", None),
            P("leaf", None, "leg", None),
            P("leaf", None, "leg", None),
            P("leaf", None, None, None, None),
            P("leaf", None, None),
        ),
        out_specs=P("leaf", None, "leg", None),
        check_vma=False,
    )
```

```python
import functools

import jax
import jax.numpy as jnp
from jax import lax
from jax.experimental import pallas as pl
from jax.experimental.pallas import tpu as pltpu
from jax.sharding import PartitionSpec as P

F32 = jnp.float32
BF16 = jnp.bfloat16
LANES = 128
VMEM_BYTES = 56 << 20
AXES = ("leaf", "leg")


def from_partner(block, axis, apart):
    count = lax.axis_size(axis)
    route = []
    for low in range(count):
        high = low | 1 << apart
        if high != low and high < count:
            route += [(low, high), (high, low)]
    return lax.ppermute(block, axis, route)


def regroup(stacked, leaf_flag_bits, leg_count):
    stacked_count, bond_size, row_count, feature_width = stacked.shape
    group_size = 2 ** len(leaf_flag_bits)
    slice_width = bond_size // (leg_count * group_size)
    shaped = stacked.reshape(
        stacked_count, leg_count, group_size, slice_width, 1, row_count, feature_width
    )
    leaf_index = lax.axis_index("leaf")
    for leaf_bit in leaf_flag_bits:
        own_bit = leaf_index >> leaf_bit & 1
        dims_now = shaped.shape
        halves = shaped.reshape(dims_now[:2] + (2, dims_now[2] // 2) + dims_now[3:])
        kept_half = lax.dynamic_index_in_dim(halves, own_bit, 2, keepdims=False)
        sent_half = lax.dynamic_index_in_dim(halves, 1 - own_bit, 2, keepdims=False)
        partner = from_partner(sent_half, "leaf", leaf_bit)
        lower_half = jnp.where(own_bit == 0, kept_half, partner)
        upper_half = jnp.where(own_bit == 0, partner, kept_half)
        joined = jnp.stack([lower_half, upper_half], axis=5)
        shaped = joined.reshape(
            dims_now[:2] + (dims_now[2] // 2, dims_now[3], dims_now[4] * 2) + dims_now[5:]
        )
    flattened = shaped.reshape(
        stacked_count, leg_count, slice_width, group_size * row_count, feature_width
    )
    regrouped = lax.all_to_all(flattened, "leg", split_axis=1, concat_axis=3, tiled=True)
    return regrouped.reshape(stacked_count, slice_width, bond_size, feature_width)


def contract_left(left_ops, tensor):
    return jnp.einsum("tlm,lra->tmra", left_ops, tensor, preferred_element_type=F32).astype(BF16)


def renormalize_level(tensor, left_ops, right_ops, leaf_flag_bits, leg_count):
    shifted_tensor = regroup(tensor[None], leaf_flag_bits, leg_count)[0]
    left_mixed = contract_left(left_ops, tensor)
    mixed_moved = regroup(left_mixed, leaf_flag_bits, leg_count)
    rotated_tensor = jnp.einsum(
        "tkra,trs->tkas", mixed_moved, right_ops, preferred_element_type=F32
    ).astype(BF16)
    partial_value = jnp.einsum(
        "tkas,ksb->tab", rotated_tensor, shifted_tensor, preferred_element_type=F32
    )
    totals = lax.psum(partial_value, "leg")
    for leaf_bit in leaf_flag_bits:
        totals = totals + from_partner(totals, "leaf", leaf_bit)
    return totals


def pair_children(operators, leaf_bit):
    side_bit = lax.axis_index("leaf") >> leaf_bit & 1
    partner = from_partner(operators, "leaf", leaf_bit)
    return (
        jnp.where(side_bit == 0, operators, partner),
        jnp.where(side_bit == 0, partner, operators),
    )


def choose_operators(operator_bank, chosen_operators, term_count):
    return [
        jnp.stack(
            [
                lax.dynamic_index_in_dim(
                    operator_bank[side], chosen_operators[term, side], 0, keepdims=False
                )
                for term in range(term_count)
            ]
        )
        for side in range(2)
    ]


def on_any_mesh(tensor_low, tensor_mid, tensor_top, child_operators, term_choice):
    leg_count = lax.axis_size("leg")
    leaf_index = lax.axis_index("leaf")
    left_ops, right_ops = choose_operators(child_operators[0], term_choice[0], term_choice.shape[1])
    level_low = renormalize_level(tensor_low[0], left_ops, right_ops, [], leg_count).astype(BF16)
    bond_size = level_low.shape[-1]
    quarter = bond_size // 4
    row_count = quarter // leg_count
    row_start = (leaf_index & 3) * quarter + lax.axis_index("leg") * row_count
    left_ops, right_ops = pair_children(level_low, 0)
    level_mid = renormalize_level(tensor_mid[0], left_ops, right_ops, [0], leg_count).astype(BF16)
    left_ops, right_ops = pair_children(level_mid, 1)
    level_top = renormalize_level(tensor_top[0], left_ops, right_ops, [1, 0], leg_count)
    return lax.dynamic_slice_in_dim(level_top, row_start, row_count, 1)[None]


def mix_kernel(chunk, starts, *refs):
    count = len(starts) - 1
    blocks, (l_ref, o_ref, lt_ref), scratch = refs[:count], refs[count : count + 3], refs[count + 3 :]
    depth, _, width = blocks[0].shape
    terms = l_ref.shape[0]
    rows = terms * depth
    pieces = width // LANES
    wide, out = scratch[:pieces], scratch[pieces:]
    at = pl.program_id(0)

    @pl.when(at == 0)
    def _():
        for t in range(terms):
            lt_ref[t * depth : (t + 1) * depth, :] = l_ref[t].astype(F32).T.astype(BF16)

    for j, block in enumerate(blocks):

        @pl.when((at >= starts[j]) & (at < starts[j + 1]))
        def _(block=block):
            for h in range(pieces):
                lanes = slice(h * LANES, (h + 1) * LANES)
                wide[h][...] = block[:, :, lanes].astype(F32).reshape(depth * chunk, LANES)

    for r in range(chunk):
        slab = jnp.concatenate(
            [wide[h][pl.ds(r, depth, stride=chunk), :].astype(BF16) for h in range(pieces)], axis=1
        )
        mixed = jnp.dot(lt_ref[...], slab, preferred_element_type=F32)
        for h in range(pieces):
            out[h][pl.ds(r, rows, stride=chunk), :] = mixed[:, h * LANES : (h + 1) * LANES]
    for h in range(pieces):
        lanes = slice(h * LANES, (h + 1) * LANES)
        value = out[h][...].reshape(terms, depth, chunk, LANES).astype(BF16)
        o_ref[:, :, :, lanes] = value


def mix(blocks, left_ops, counts=None, chunk=8):
    counts = counts or [block.shape[1] for block in blocks]
    depth, _, width = blocks[0].shape
    terms = left_ops.shape[0]
    pieces = width // LANES
    starts = [0]
    for rows in counts:
        starts.append(starts[-1] + rows // chunk)
    total = starts[-1] * chunk

    def spec(j):
        first, last = starts[j], starts[j + 1] - 1
        return pl.BlockSpec(
            (depth, chunk, width), lambda i: (0, jnp.clip(i, first, last) - first, 0)
        )

    return pl.pallas_call(
        functools.partial(mix_kernel, chunk, tuple(starts)),
        out_shape=jax.ShapeDtypeStruct((terms, depth, total, width), BF16),
        grid=(starts[-1],),
        in_specs=[spec(j) for j in range(len(blocks))]
        + [pl.BlockSpec(left_ops.shape, lambda i: (0, 0, 0))],
        out_specs=pl.BlockSpec((terms, depth, chunk, width), lambda i: (0, 0, i, 0)),
        scratch_shapes=[pltpu.VMEM((terms * depth, depth), BF16)]
        + [pltpu.VMEM((depth * chunk, LANES), F32)] * pieces
        + [pltpu.VMEM((terms * depth * chunk, LANES), F32)] * pieces,
        compiler_params=pltpu.CompilerParams(vmem_limit_bytes=VMEM_BYTES),
        cost_estimate=pl.CostEstimate(
            flops=3 * 2 * terms * depth * depth * total * width,
            bytes_accessed=(1 + terms) * 2 * depth * total * width,
            transcendentals=0,
        ),
    )(*blocks, left_ops)


def combine_kernel(block_count, mixed_count, group, *refs):
    blocks = refs[:block_count]
    mixed = refs[block_count : block_count + mixed_count]
    r_ref, rows_ref, columns_ref, o_ref, turn_ref = refs[block_count + mixed_count :]
    terms, step = mixed[0].shape[:2]
    own = turn_ref.shape[0] // terms

    @pl.when(pl.program_id(0) == 0)
    def _():
        o_ref[...] = jnp.zeros_like(o_ref)
        for t in range(terms):
            picked = jnp.dot(rows_ref[...], r_ref[t], preferred_element_type=F32).astype(BF16)
            turn_ref[t * own : (t + 1) * own, :] = jnp.dot(
                picked, columns_ref[...], preferred_element_type=F32
            ).astype(BF16)

    for start in range(0, step, group):
        members = range(start, start + group)
        turned = []
        for m in members:
            whole = jnp.concatenate([block[m] for block in blocks], axis=0)
            turned.append(
                jnp.dot(turn_ref[...], whole, preferred_element_type=F32).astype(BF16)
            )
        for t in range(terms):
            left = jnp.concatenate([x[t, m] for m in members for x in mixed], axis=0)
            right = jnp.concatenate([y[t * own : (t + 1) * own] for y in turned], axis=0)
            o_ref[t] += lax.dot_general(
                left, right, (((0,), (0,)), ((), ())), preferred_element_type=F32
            )


def combine(blocks, mixed, right_ops, row_pick, column_pick, step=32, group=8):
    depth, _, width = blocks[0].shape
    terms = right_ops.shape[0]
    own = row_pick.shape[0]
    return pl.pallas_call(
        functools.partial(combine_kernel, len(blocks), len(mixed), group),
        out_shape=jax.ShapeDtypeStruct((terms, width, width), F32),
        grid=(depth // step,),
        in_specs=[pl.BlockSpec((step,) + b.shape[1:], lambda i: (i, 0, 0)) for b in blocks]
        + [pl.BlockSpec((terms, step) + x.shape[2:], lambda i: (0, i, 0, 0)) for x in mixed]
        + [
            pl.BlockSpec(right_ops.shape, lambda i: (0, 0, 0)),
            pl.BlockSpec(row_pick.shape, lambda i: (0, 0)),
            pl.BlockSpec(column_pick.shape, lambda i: (0, 0)),
        ],
        out_specs=pl.BlockSpec((terms, width, width), lambda i: (0, 0, 0)),
        scratch_shapes=[pltpu.VMEM((terms * own, depth), BF16)],
        compiler_params=pltpu.CompilerParams(vmem_limit_bytes=VMEM_BYTES),
        cost_estimate=pl.CostEstimate(
            flops=2 * terms * own * depth * width * (depth + width),
            bytes_accessed=2 * depth * width * (depth + terms * own),
            transcendentals=0,
        ),
    )(*blocks, *mixed, right_ops, row_pick, column_pick)


def move(array, route):
    leg_count = lax.axis_size("leg")
    pairs = [(a * leg_count + g, b * leg_count + h) for (a, g), (b, h) in route.items()]
    return lax.ppermute(array, AXES, pairs)


def hop(array, start, end):
    return move(array, {(n, start): (n, end) for n in range(lax.axis_size("leaf"))})


def toward(array, start, end, sinks):
    leaves = range(lax.axis_size("leaf"))
    return move(array, {(n, s ^ start): (n, s ^ end) for n in leaves for s in sinks})


def swap(array, apart, sinks):
    leaves = range(lax.axis_size("leaf"))
    return move(array, {(n, s): (n ^ apart, s) for n in leaves for s in sinks})


def add_core(partial, sinks):
    return (partial + swap(partial, 1, sinks)).astype(BF16)


def picks(index, own):
    size = index.shape[0]
    canonical = jnp.arange(size)
    rows = (index[:own, None] == canonical[None, :]).astype(BF16)
    columns = (canonical[:, None] == index[None, :]).astype(BF16)
    return rows, columns


def order(bond_size, parts, leg_count, own_part, legs):
    width = bond_size // (leg_count * len(parts))
    place = jnp.arange(bond_size)
    part_at = place // (leg_count * width)
    part = sum(jnp.where(part_at == i, own_part ^ p, 0) for i, p in enumerate(parts))
    leg_at = place // width % leg_count
    leg = sum(jnp.where(leg_at == i, g, 0) for i, g in enumerate(legs))
    return leg * (bond_size // leg_count) + part * width + place % width


def top_picks(leaf, bond_size, leg_count, sink):
    width = bond_size // (leg_count * 4)
    place = jnp.arange(bond_size)
    core_at, leg_at = place // (leg_count * 2 * width), place // (2 * width) % leg_count
    plane_at = place // width % 2
    part = (leaf & 3) ^ core_at ^ 2 * plane_at
    index = (sink ^ leg_at) * (bond_size // leg_count) + part * width + place % width
    columns = picks(index, bond_size)[1]
    own = order(bond_size, (0, 1, 2, 3), leg_count, leaf & 3, [sink ^ d for d in range(leg_count)])
    return picks(own, bond_size // 4)[0], columns


def halves(block):
    middle = block.shape[1] // 2
    return block[:, :middle], block[:, middle:]


def on_square(tensor_low, tensor_mid, tensor_top, child_operators, term_choice):
    leaf, leg = lax.axis_index("leaf"), lax.axis_index("leg")
    leaf_count, leg_count = lax.axis_size("leaf"), lax.axis_size("leg")
    leaves, legs = range(leaf_count), range(leg_count)
    low, mid, top = tensor_low[0], tensor_mid[0], tensor_top[0]
    bond_size = low.shape[-1]
    core = leaf & 1
    low_sinks, mid_sinks, top_sinks = (0, 3), (1,), (2,)

    half = low.shape[1] // 2
    own_half = lax.dynamic_slice_in_dim(low, core * half, half, 1)
    sent_half = lax.dynamic_slice_in_dim(low, (1 - core) * half, half, 1)
    got_half = swap(sent_half, 1, legs)
    top_other = swap(top, 2, legs)
    own_first = (core == 0) == (leg < 2)
    second = [jnp.where(own_first, g, o) for g, o in zip(halves(got_half), halves(own_half))]
    low_bent = toward(second[1], 3, 1, low_sinks)
    low_straight = toward(second[0], 3, 0, low_sinks)
    first = jnp.where(own_first, own_half, got_half)
    low_x = toward(first, 1, 0, low_sinks)
    low_y0 = toward(second[0], 2, 0, low_sinks)
    low_y1 = toward(second[1], 2, 0, low_sinks)
    low_bent = toward(low_bent, 1, 0, low_sinks)
    low_column = [first, low_x, low_y0, low_y1, low_straight, low_bent]
    low_blocks = low_column + [swap(block, 1, low_sinks) for block in low_column]
    mid_column = [mid] + [toward(mid, d, 0, mid_sinks) for d in (1, 2, 3)]
    mid_blocks = mid_column + [swap(block, 1, mid_sinks) for block in mid_column]
    wide_top = jnp.concatenate([top, top_other], axis=1)
    top_column = [wide_top] + [toward(wide_top, d, 0, top_sinks) for d in (1, 2, 3)]
    top_blocks = top_column + [swap(block, 1, top_sinks) for block in top_column]

    left_ops, right_ops = choose_operators(child_operators[0], term_choice[0], term_choice.shape[1])
    ops_pair = jnp.stack([left_ops, right_ops])
    other_pair = swap(ops_pair, 1, low_sinks)
    left_ops, right_ops = jnp.where(core != leg // 2, other_pair, ops_pair)
    low_legs = [leg, leg ^ 1, leg ^ 2, leg ^ 3]
    row_pick, column_pick = picks(
        order(bond_size, (0, 1), leg_count, core, low_legs), bond_size // 2
    )
    mixed = [
        mix(low_column[:1], left_ops), mix(low_column[1:2], left_ops), mix(low_column[2:], left_ops)
    ]
    partial = combine(low_blocks, mixed, right_ops, row_pick, column_pick)
    ops_low = add_core(partial, low_sinks)

    sink = mid_sinks[0]
    left_ops = hop(ops_low, low_sinks[0], sink)
    right_ops = hop(ops_low, low_sinks[1], sink)
    row_pick, column_pick = picks(
        order(bond_size, (0, 1), leg_count, core, [sink ^ d for d in range(4)]), bond_size // 2
    )
    mixed = [mix(mid_column[:3], left_ops), mix(mid_column[3:], left_ops)]
    partial = combine(mid_blocks, mixed, right_ops, row_pick, column_pick)
    ops_mid = add_core(partial, mid_sinks)

    sink = top_sinks[0]
    near = hop(ops_mid, mid_sinks[0], sink)
    across = move(ops_mid, {(n, mid_sinks[0]): (n ^ 2, sink) for n in leaves})
    upper = (leaf >> 1 & 1) == 1
    left_ops, right_ops = jnp.where(upper, across, near), jnp.where(upper, near, across)
    row_pick, column_pick = top_picks(leaf, bond_size, leg_count, sink)
    mixed = [mix(top_column, left_ops, [top.shape[1]] * len(top_column))]
    partial = combine(top_blocks, mixed, right_ops, row_pick, column_pick)

    quarter = bond_size // 4
    summed = lax.dynamic_slice_in_dim(partial, (leaf & 3) * quarter, quarter, 1)
    for apart in (1, 2, 3):
        piece = lax.dynamic_slice_in_dim(partial, ((leaf & 3) ^ apart) * quarter, quarter, 1)
        summed = summed + swap(piece, apart, top_sinks)
    rows = quarter // leg_count
    result = jnp.where(leg == sink, summed[:, sink * rows : (sink + 1) * rows], 0)
    for g in legs:
        if g != sink:
            result = result + hop(summed[:, g * rows : (g + 1) * rows], sink, g)
    return result[None]


def is_square(mesh):
    return mesh.shape["leg"] == 4 and mesh.shape["leaf"] % 4 == 0


def solution(mesh):
    square = is_square(mesh)

    def on_device(*arguments):
        return on_square(*arguments) if square else on_any_mesh(*arguments)

    return jax.shard_map(
        on_device,
        mesh=mesh,
        in_specs=(
            P("leaf", None, "leg", None),
            P("leaf", None, "leg", None),
            P("leaf", None, "leg", None),
            P("leaf", None, None, None, None),
            P("leaf", None, None),
        ),
        out_specs=P("leaf", None, "leg", None),
        check_vma=False,
    )
```
